32 devices in a mesh: section: 4 (over z), expert: 8 (over y, x, core).
Axes of the slice: x: 2, y: 2, z: 4, core: 2. Of those that a mesh axis runs over, the one named last changes fastest.
Arguments:
- tokens: bfloat16 [96, 3584], P('expert', 'section'), may hold values from -6 to 6
- scales: float32 [96, 28], P('expert'), may hold values from 0.25 to 4
- expert_ids: int32 [96, 8], P('expert'), may hold values from 0 to 63, all different within a row; in each aligned block of 12 rows (0 to 11, 12 to 23, ...) at most 2 rows name the same one
- gate_fixed: int32 [96, 8], P('expert'), may hold values from 1 to 65535
- w_gate: bfloat16 [64, 3584, 2048], P('expert', None, 'section'), may hold values from -0.09375 to 0.09375
- w_up: bfloat16 [64, 3584, 2048], P('expert', None, 'section'), may hold values from -0.09375 to 0.09375
- w_down: bfloat16 [64, 2048, 3584], P('expert', 'section'), may hold values from -0.125 to 0.125
Outputs:
- mixed: bfloat16 [96, 3584], P('expert', 'section')
The draws below stay inside these ranges and needn't reach their ends.
Inputs may be any that keep to these rules, and one draw needn't show every extreme that they name: `expert_ids`: each row names 8 different experts. Among the 12 rows of one device (aligned blocks of 12 rows) no expert is named more than 2 times; in some block some expert is named exactly 2 times.
All inputs are finite; a program needn't handle non-finite values.
Results may differ from the reference program's by a relative error of at most 0.018.
Values may be sent and summed in bfloat16 or wider, within the bound.
A program may use at most 192 MiB of HBM per device.

```python
import math
import jax
import jax.numpy as jnp
import numpy as np
from jax import lax

D = 3584
FF = 2048
EXPERTS = 64
TOPK = 8
TOK_DEV = 12
CAP = 2
TOKENS = 96
N_SECTION = 4
N_EXPERT = 8


def with_ends(array, own_key, smallest, top_value):
    longest = array.shape.index(max(array.shape))
    spots = []
    for shift in (0, 1):
        where = [jax.random.randint(jax.random.fold_in(own_key, axis), (), 0, length) for axis, length in enumerate(array.shape)]
        where[longest] = (where[longest] + shift) % array.shape[longest]
        spots.append(tuple(where))
    return array.at[spots[0]].set(smallest).at[spots[1]].set(top_value)


def level_of(stream_key, extent, shards, least, largest):
    def one(dim, shards_of):
        steps = jax.random.uniform(jax.random.fold_in(jax.random.fold_in(stream_key, 6), dim), (shards_of,), jnp.float32, least / len(shards), largest / len(shards))
        return jnp.repeat(jnp.exp(steps), extent[dim] // shards_of).reshape((-1,) + (1,) * (len(extent) - dim - 1))

    loudness = one(*shards[0])
    for cut in shards[1:]:
        loudness = loudness * one(*cut)
    return loudness


def shared_out(stream_key, own, number, rows, number_of, top, most, slope):
    sequence = jax.random.permutation(stream_key, number_of)
    crowded, usual = shares(number_of, rows * top, most, slope, True), shares(number_of, rows * top, most, slope, False)
    places = jnp.arange(number_of)

    def named(sizes, turn):
        used = int((sizes > 0).sum())
        fixed = max(1, used // 4)
        passed = fixed + (places - fixed + turn * (used - fixed)) % max(1, number_of - fixed)
        return jnp.zeros((number_of,), jnp.int32).at[sequence[jnp.where(places < fixed, places, passed)]].set(jnp.asarray(sizes, jnp.int32))

    sizes = jnp.where(number % 4 == 0, named(crowded, number // 4), named(usual, number - number // 4 - 1))
    mixed = jax.random.permutation(jax.random.fold_in(own, 3), number_of)
    giver, sink = mixed[0:number_of // 2 * 2:2], mixed[1:number_of // 2 * 2:2]
    margin = jnp.minimum(sizes[giver] - 1, most - sizes[sink]) // 2
    margin = jnp.where((giver == sequence[0]) | (sink == sequence[0]) | (sizes[sink] == 0), 0, jnp.maximum(margin, 0))
    passed = jax.random.randint(jax.random.fold_in(own, 4), (number_of // 2,), 0, 1 << 20) % (margin + 1)
    sizes = sizes.at[giver].add(-passed).at[sink].add(passed)
    members = jnp.searchsorted(jnp.cumsum(sizes), jnp.arange(rows * top), side="right").astype(jnp.int32)
    table = members.reshape(top, rows).T
    table = table[jax.random.permutation(jax.random.fold_in(own, 1), rows)]
    turn = jax.random.randint(jax.random.fold_in(own, 2), (rows, 1), 0, top)
    return jnp.take_along_axis(table, (jnp.arange(top)[None, :] + turn) % top, axis=1)


def shares(number_of, total, most, lean, full):
    portions = [(1 << 20) // math.isqrt(rank ** lean) + 1 for rank in range(1, number_of + 1)]
    largest = most if full else min(most, max(-(-total // number_of), total * portions[0] // sum(portions)))
    least = 1 if total - largest >= number_of - 1 else 0
    counts, spare = [largest] + [least] * (number_of - 1), total - largest - least * (number_of - 1)
    while spare > 0:
        movable = [i for i in range(1, number_of) if counts[i] < largest] or [i for i in range(1, number_of) if counts[i] < most]
        pool, remaining = sum([portions[i] for i in movable]), spare
        for i in movable:
            extra = min(most - counts[i], max(1, remaining * portions[i] // pool), spare)
            counts[i] = counts[i] + extra
            spare = spare - extra
    return np.array(counts)


def scatter_about(own_key, dims, scale, limit, pieces=(), held_as=jnp.bfloat16):
    factor_of = level_of(own_key, dims, pieces, -0.22, 0.18) if pieces else 1.0
    entries = jax.random.normal(own_key, dims, jnp.float32) * scale * factor_of
    return jnp.minimum(jnp.maximum(entries, -limit), limit).astype(held_as)


def setup_inputs(seed: int = 0) -> dict:
    key_of = jax.random.split(jax.random.key(seed), 8)
    tokens = scatter_about(key_of[0], (TOKENS, D), 1.0, 6.0, ((0, 8), (1, 4)))
    scales = jnp.clip(jnp.exp(math.log(4.0) - 2.7725887 * jax.random.uniform(key_of[1], (TOKENS, D // 128), jnp.float32) ** level_of(key_of[1], (TOKENS, D // 128), ((0, 8),), -0.2, 0.2)), 0.25, 4.0)
    expert_ids_keys = jax.random.split(jax.random.fold_in(key_of[2], 1), TOKENS // TOK_DEV)
    expert_ids_turns = jax.random.permutation(jax.random.fold_in(key_of[2], 3), TOKENS // TOK_DEV)
    expert_ids = jax.vmap(lambda own, number: shared_out(jax.random.fold_in(key_of[2], 2), own, number, TOK_DEV, EXPERTS, TOPK, CAP, 2))(expert_ids_keys, expert_ids_turns).reshape((TOKENS, TOPK))
    gate_fixed = with_ends(jax.random.randint(key_of[3], (TOKENS, TOPK), 1, 65536), jax.random.fold_in(key_of[3], 1), 1, 65535).astype(jnp.int32)
    w_gate = scatter_about(key_of[4], (EXPERTS, D, FF), D ** -0.5, 0.09375, ((0, 8), (2, 4)))
    w_up = scatter_about(key_of[5], (EXPERTS, D, FF), D ** -0.5, 0.09375, ((0, 8), (2, 4)))
    w_down = scatter_about(key_of[6], (EXPERTS, FF, D), FF ** -0.5, 0.125, ((0, 8), (1, 4)))
    return {"tokens": tokens, "scales": scales, "expert_ids": expert_ids, "gate_fixed": gate_fixed, "w_gate": w_gate, "w_up": w_up, "w_down": w_down}


def reference(tokens, scales, expert_ids, gate_fixed, w_gate, w_up, w_down):
    blocks = D // 128
    dequant = (tokens.astype(jnp.float32).reshape(TOKENS, blocks, 128) * scales[:, :, None]).reshape(TOKENS, D).astype(jnp.bfloat16)
    routes = TOK_DEV * TOPK
    grouped = expert_ids.reshape(N_EXPERT, routes)
    onehot = (grouped[:, :, None] == jnp.arange(EXPERTS, dtype=jnp.int32)[None, None, :]).astype(jnp.int32)
    earlier = (jnp.cumsum(onehot, axis=1) - onehot).astype(jnp.int32)
    position = jnp.sum(earlier * onehot, axis=2).astype(jnp.int32)
    slot_rows = N_EXPERT * CAP
    within = (jnp.arange(N_EXPERT, dtype=jnp.int32)[:, None] * CAP + position).astype(jnp.int32)
    source = jnp.broadcast_to(jnp.arange(TOKENS, dtype=jnp.int32).reshape(N_EXPERT, TOK_DEV, 1), (N_EXPERT, TOK_DEV, TOPK)).reshape(N_EXPERT, routes)
    slot_table = jnp.zeros((EXPERTS, slot_rows), jnp.int32).at[grouped.reshape(-1), within.reshape(-1)].set((source.reshape(-1) + 1).astype(jnp.int32))
    padded = jnp.concatenate([jnp.zeros((1, D), jnp.bfloat16), dequant], axis=0)
    slice_width = FF // N_SECTION

    def one_expert(operands):
        row_index, gate_w, up_w, down_w = operands
        gathered = padded[row_index]
        gate_part = jnp.dot(gathered, gate_w, preferred_element_type=jnp.float32)
        up_part = jnp.dot(gathered, up_w, preferred_element_type=jnp.float32)
        hidden = (jax.nn.silu(gate_part) * up_part).astype(jnp.bfloat16).reshape(slot_rows, N_SECTION, slice_width)
        section_parts = jnp.einsum("rsf,sfd->srd", hidden.astype(jnp.float32), down_w.reshape(N_SECTION, slice_width, D).astype(jnp.float32))
        rounded = lax.optimization_barrier(section_parts.astype(jnp.bfloat16))
        return jnp.sum(rounded.astype(jnp.float32), axis=0)

    outputs = lax.map(one_expert, (slot_table, w_gate, w_up, w_down)).reshape(EXPERTS * slot_rows, D)
    row_index = (grouped * slot_rows + within).reshape(TOKENS, TOPK).astype(jnp.int32)
    picked = outputs[row_index]
    weights = gate_fixed.astype(jnp.float32) * (1.0 / 65536.0)
    return jnp.sum(picked * weights[:, :, None], axis=1).astype(jnp.bfloat16)
```

```python
import functools

import jax
import jax.numpy as jnp
from jax import lax
from jax.experimental import pallas as pl
from jax.experimental.pallas import tpu as pltpu
from jax.sharding import PartitionSpec as P


def shards(tokens, scales, expert_ids, gate_fixed, w_gate, w_up, w_down):
    n_expert = lax.axis_size("expert")
    tok_rows, local_width = tokens.shape
    block_count = scales.shape[1]
    top_count = expert_ids.shape[1]
    exp_local = w_gate.shape[0]
    experts_all = exp_local * n_expert
    capacity = tok_rows // 6
    column_ids = lax.axis_index("section") * local_width + jnp.arange(local_width, dtype=jnp.int32)
    block_table = (
        jnp.arange(block_count, dtype=jnp.int32)[:, None] == (column_ids // 128)[None, :]
    ).astype(jnp.float32)
    scale_cols = jnp.dot(scales, block_table, precision=lax.Precision.HIGHEST)
    dequant = (tokens.astype(jnp.float32) * scale_cols).astype(jnp.bfloat16)
    flat_ids = expert_ids.reshape(-1)
    onehot = (flat_ids[:, None] == jnp.arange(experts_all, dtype=jnp.int32)[None, :]).astype(
        jnp.int32
    )
    earlier = jnp.cumsum(onehot, axis=0) - onehot
    position = jnp.sum(earlier * onehot, axis=1)
    slot_flat = (flat_ids * capacity + position).reshape(tok_rows, top_count)
    chooser = jnp.any(
        jnp.arange(experts_all * capacity, dtype=jnp.int32)[:, None, None] == slot_flat[None, :, :],
        axis=2,
    ).astype(jnp.bfloat16)
    outgoing = jnp.dot(chooser, dequant, preferred_element_type=jnp.float32).astype(jnp.bfloat16)
    outgoing = outgoing.reshape(n_expert, exp_local, capacity, local_width)
    whole = lax.all_gather(
        lax.all_to_all(outgoing, "expert", split_axis=0, concat_axis=0, tiled=True),
        "section",
        axis=3,
        tiled=True,
    )
    gate_part = jnp.einsum("seld,edf->self", whole, w_gate, preferred_element_type=jnp.float32)
    up_part = jnp.einsum("seld,edf->self", whole, w_up, preferred_element_type=jnp.float32)
    hidden = (jax.nn.silu(gate_part) * up_part).astype(jnp.bfloat16)
    partial_rows = jnp.einsum(
        "self,efd->seld", hidden, w_down, preferred_element_type=jnp.float32
    ).astype(jnp.bfloat16)
    weights = gate_fixed.astype(jnp.float32) * (1.0 / 65536.0)
    summed = lax.psum_scatter(
        partial_rows.astype(jnp.float32).astype(jnp.bfloat16),
        "section",
        scatter_dimension=3,
        tiled=True,
    ).astype(jnp.float32)
    returned = lax.all_to_all(
        summed.astype(jnp.bfloat16), "expert", split_axis=0, concat_axis=0, tiled=True
    ).astype(summed.dtype)
    returned = returned.reshape(experts_all * capacity, returned.shape[3])
    picked = returned[slot_flat]
    return jnp.sum(picked * weights[:, :, None], axis=1).astype(jnp.bfloat16)


MESH = pl.DeviceIdType.MESH
VMEM_BYTES = 67043328
HALVES = 2


def layer_kernel(
    n_sec, n_exp, depth,
    tok_ref, sc_ref, id_ref, gf_ref, wg_ref, wu_ref, wd_ref, o_ref,
    gbuf, ubuf, dbuf, xg, x2, gates, gates2, hid, acc, part, landed, sect, sect_in,
    w_sem, d_sem, z_send, z_recv, p_send, p_recv, c_send, c_recv, g_send, g_recv,
    a_send, a_recv, b_send, b_recv,
):
    sec, me = lax.axis_index("section"), lax.axis_index("expert")
    rows, width = tok_ref.shape
    exp_local, features, hidden = wg_ref.shape
    pad = x2.shape[0] // n_exp
    per_half = exp_local // HALVES
    sib = me + 1 - 2 * lax.rem(me, 2)
    peers = [lax.rem(me + d, n_exp) for d in range(n_exp)]
    senders = [lax.rem(me + n_exp - d, n_exp) for d in range(n_exp)]

    def gate_copy(e):
        slot = lax.rem(e, depth)
        return pltpu.make_async_copy(wg_ref.at[e], gbuf.at[slot], w_sem.at[slot, 0])

    def up_copy(e):
        slot = lax.rem(e, depth)
        return pltpu.make_async_copy(wu_ref.at[e], ubuf.at[slot], w_sem.at[slot, 1])

    def down_copy(half, c):
        column = pl.multiple_of(lax.rem(sec + 1 + c, n_sec) * width, 128)
        return pltpu.make_async_copy(
            wd_ref.at[pl.ds(half * per_half, per_half), :, pl.ds(column, width)],
            dbuf.at[c],
            d_sem.at[c],
        )

    for e in range(per_half):
        gate_copy(e).start()
        up_copy(e).start()
    for c in range(n_sec):
        down_copy(0, c).start()
    for e in range(per_half, depth):
        gate_copy(e).start()
        up_copy(e).start()

    barrier = pltpu.get_barrier_semaphore()
    for d in range(1, n_sec):
        pl.semaphore_signal(
            barrier, inc=1, device_id=(lax.rem(sec + d, n_sec), me), device_id_type=MESH
        )
    for d in range(1, n_exp):
        pl.semaphore_signal(barrier, inc=1, device_id=(sec, peers[d]), device_id_type=MESH)

    scales = sc_ref[...]
    block_ids = lax.broadcasted_iota(jnp.int32, scales.shape, 1)
    for j in range(width // 128):
        block = sec * (width // 128) + j
        scale = jnp.sum(jnp.where(block_ids == block, scales, 0.0), axis=1, keepdims=True)
        cols = slice(j * 128, (j + 1) * 128)
        xg[me, sec, :, cols] = (tok_ref[:, cols].astype(jnp.float32) * scale).astype(jnp.bfloat16)
    ids = id_ref[...]
    weights = gf_ref[...].astype(jnp.float32) * (1.0 / 65536.0)
    expert_row = lax.broadcasted_iota(jnp.int32, gates.shape[1:], 1)
    table = jnp.zeros(gates.shape[1:], jnp.float32)
    for k in range(ids.shape[1]):
        table = table + jnp.where(expert_row == ids[:, k : k + 1], weights[:, k : k + 1], 0.0)
    gates[me] = table
    x2[...] = jnp.zeros_like(x2)
    gates2[...] = jnp.zeros_like(gates2)

    pl.semaphore_wait(barrier, n_sec - 1 + n_exp - 1)

    def z_copy(d):
        return pltpu.make_async_remote_copy(
            xg.at[me, sec], xg.at[me, sec], z_send.at[d], z_recv.at[d],
            device_id=(lax.rem(sec + d, n_sec), me), device_id_type=MESH,
        )

    def z_in(d):
        slot = xg.at[me, lax.rem(sec + n_sec - d, n_sec)]
        return pltpu.make_async_remote_copy(
            slot, slot, z_send.at[d], z_recv.at[d],
            device_id=(lax.rem(sec + d, n_sec), me), device_id_type=MESH,
        )

    def move(block, send, recv, to):
        return pltpu.make_async_remote_copy(
            block, block, send, recv, device_id=(sec, to), device_id_type=MESH
        )

    def gate_move(block, d):
        return move(gates.at[block], g_send.at[d], g_recv.at[d], peers[d])

    chips = list(range(2, n_exp, 2))
    for d in range(1, n_sec):
        z_copy(d).start()
    for d in range(1, n_exp):
        gate_move(me, d).start()
    for d in range(1, n_sec):
        z_in(d).wait_recv()
    for d in chips:
        move(xg.at[me], p_send.at[d], p_recv.at[d], peers[d]).start()
    move(xg.at[me], c_send.at[0], c_recv.at[0], sib).start()
    for d in chips:
        block = xg.at[senders[d]]
        move(block, p_send.at[d], p_recv.at[d], peers[d]).wait_recv()
        move(block, c_send.at[d], c_recv.at[d], sib).start()
    for d in [0] + chips:
        block = xg.at[lax.rem(sib + n_exp - d, n_exp)]
        move(block, c_send.at[d], c_recv.at[d], sib).wait_recv()
    for d in range(1, n_exp):
        gate_move(senders[d], d).wait_recv()

    for b in range(n_exp):
        for s in range(n_sec):
            x2[b * pad : b * pad + rows, s * width : (s + 1) * width] = xg[b, s]
        gates2[b * pad : b * pad + rows, :] = gates[b]

    def expert(e, half):
        slot = lax.rem(e, depth)
        gate_copy(e).wait()
        up_copy(e).wait()
        lanes = lax.broadcasted_iota(jnp.int32, gates2.shape, 1)
        chosen = jnp.sum(
            jnp.where(lanes == me * exp_local + e, gates2[...], 0.0), axis=1, keepdims=True
        )
        step = TILE if hidden % TILE == 0 else hidden
        for n in range(0, hidden, step):
            gate = jnp.dot(
                x2[...], gbuf[slot, :, n : n + step], preferred_element_type=jnp.float32
            )
            up = jnp.dot(x2[...], ubuf[slot, :, n : n + step], preferred_element_type=jnp.float32)
            value = (jax.nn.silu(gate) * up * chosen).astype(jnp.bfloat16)
            hid[:, pl.ds(pl.multiple_of((e - half * per_half) * hidden + n, 128), step)] = value

        @pl.when(e + depth < exp_local)
        def _():
            gate_copy(e + depth).start()
            up_copy(e + depth).start()

    def product(c):
        down = dbuf[c].reshape(per_half * hidden, width)
        return jnp.dot(hid[...], down, preferred_element_type=jnp.float32)

    @pl.loop(0, per_half)
    def _(e):
        expert(e, 0)

    @pl.loop(0, n_sec)
    def _(c):
        down_copy(0, c).wait()
        acc[c] = product(c)
        down_copy(1, c).start()

    @pl.loop(per_half, exp_local)
    def _(e):
        expert(e, 1)

    def a_copy(c, d):
        return pltpu.make_async_remote_copy(
            part.at[c, peers[d]], landed.at[c, me], a_send.at[c, d], a_recv.at[c, d],
            device_id=(sec, peers[d]), device_id_type=MESH,
        )

    def a_in(c, d):
        return pltpu.make_async_remote_copy(
            part.at[c, peers[d]], landed.at[c, senders[d]], a_send.at[c, d], a_recv.at[c, d],
            device_id=(sec, peers[d]), device_id_type=MESH,
        )

    def b_copy(c):
        return pltpu.make_async_remote_copy(
            sect.at[c], sect_in.at[c], b_send.at[c], b_recv.at[c],
            device_id=(lax.rem(sec + 1 + c, n_sec), me), device_id_type=MESH,
        )

    def over_experts(c):
        total = part[c, me].astype(jnp.float32)
        for d in range(1, n_exp):
            a_in(c, d).wait_recv()
            total = total + landed[c, senders[d]].astype(jnp.float32)
        return total

    @pl.loop(0, n_sec)
    def _(c):
        down_copy(1, c).wait()
        acc[c] = acc[c] + product(c)
        for b in range(n_exp):
            part[c, b] = acc[c, b * pad : b * pad + rows, :].astype(jnp.bfloat16)
        for d in range(1, n_exp):
            a_copy(c, d).start()

        @pl.when(c >= 1)
        def _():
            sect[c - 1] = over_experts(c - 1).astype(jnp.bfloat16)
            b_copy(c - 1).start()

    total = over_experts(n_sec - 1)
    for c in range(n_sec - 1):
        b_copy(c).wait_recv()
        total = total + sect_in[c].astype(jnp.float32)
    o_ref[...] = total.astype(o_ref.dtype)

    for d in range(1, n_sec):
        z_copy(d).wait_send()
    for d in range(1, n_exp):
        gate_move(me, d).wait_send()
    for d in chips:
        move(xg.at[me], p_send.at[d], p_recv.at[d], peers[d]).wait_send()
        move(xg.at[senders[d]], c_send.at[d], c_recv.at[d], sib).wait_send()
    move(xg.at[me], c_send.at[0], c_recv.at[0], sib).wait_send()

    @pl.loop(0, n_sec)
    def _(c):
        for d in range(1, n_exp):
            a_copy(c, d).wait_send()

    @pl.loop(0, n_sec - 1)
    def _(c):
        b_copy(c).wait_send()


TILE = 256


def sizes(n_sec, n_exp, tokens, w_gate, experts_all):
    rows, width = tokens.shape
    exp_local, features, hidden = w_gate.shape
    pad = -(-rows // 16) * 16
    half = exp_local // HALVES
    scratch = [
        ((n_exp, n_sec, rows, width), jnp.bfloat16),
        ((n_exp * pad, features), jnp.bfloat16),
        ((n_exp, rows, experts_all), jnp.float32),
        ((n_exp * pad, experts_all), jnp.float32),
        ((n_exp * pad, half * hidden), jnp.bfloat16),
        ((n_sec, n_exp * pad, width), jnp.float32),
        ((n_sec, n_exp, rows, width), jnp.bfloat16),
        ((n_sec, n_exp, rows, width), jnp.bfloat16),
        ((n_sec - 1, rows, width), jnp.bfloat16),
        ((n_sec - 1, rows, width), jnp.bfloat16),
    ]
    return pad, scratch


def fused(tokens, scales, expert_ids, gate_fixed, w_gate, w_up, w_down):
    n_sec, n_exp = lax.axis_size("section"), lax.axis_size("expert")
    rows, width = tokens.shape
    exp_local, features, hidden = w_gate.shape
    half = exp_local // HALVES
    pad, scratch = sizes(n_sec, n_exp, tokens, w_gate, exp_local * n_exp)
    used = 0
    for shape, kind in scratch:
        lead = 1
        for extent in shape[:-2]:
            lead *= extent
        used += lead * (-(-shape[-2] // 16) * 16) * (-(-shape[-1] // 128) * 128) * jnp.dtype(kind).itemsize
    used += 2 * n_sec * half * hidden * width + SPARE
    depth = min(exp_local, (VMEM_BYTES - used) // (4 * features * hidden))
    dma = pltpu.SemaphoreType.DMA
    vmem, anyspace = pl.BlockSpec(memory_space=pltpu.VMEM), pl.BlockSpec(memory_space=pl.ANY)
    return pl.pallas_call(
        functools.partial(layer_kernel, n_sec, n_exp, depth),
        out_shape=jax.ShapeDtypeStruct((rows, width), jnp.bfloat16),
        in_specs=[vmem] * 4 + [anyspace] * 3,
        out_specs=vmem,
        scratch_shapes=[
            pltpu.VMEM((depth, features, hidden), jnp.bfloat16),
            pltpu.VMEM((depth, features, hidden), jnp.bfloat16),
            pltpu.VMEM((n_sec, half, hidden, width), jnp.bfloat16),
        ]
        + [pltpu.VMEM(shape, kind) for shape, kind in scratch]
        + [
            dma((depth, 2)), dma((n_sec,)),
            dma((n_sec,)), dma((n_sec,)),
            dma((n_exp,)), dma((n_exp,)), dma((n_exp,)), dma((n_exp,)),
            dma((n_exp,)), dma((n_exp,)),
            dma((n_sec, n_exp)), dma((n_sec, n_exp)),
            dma((n_sec - 1,)), dma((n_sec - 1,)),
        ],
        compiler_params=pltpu.CompilerParams(
            collective_id=0, has_side_effects=True, vmem_limit_bytes=VMEM_BYTES
        ),
    )(tokens, scales, expert_ids, gate_fixed, w_gate, w_up, w_down)


SPARE = 1 << 20


def layer(tokens, scales, expert_ids, gate_fixed, w_gate, w_up, w_down):
    n_exp = lax.axis_size("expert")
    width = tokens.shape[1]
    exp_local, _, hidden = w_gate.shape
    fits = width % 128 == 0 and hidden % 128 == 0 and exp_local % HALVES == 0 and n_exp <= 16
    body = fused if fits and n_exp % 2 == 0 else shards
    return body(tokens, scales, expert_ids, gate_fixed, w_gate, w_up, w_down)


def solution(mesh):
    placed = (
        P("expert", "section"),
        P("expert", None),
        P("expert", None),
        P("expert", None),
        P("expert", None, "section"),
        P("expert", None, "section"),
        P("expert", "section", None),
    )
    return jax.shard_map(
        layer, mesh=mesh, in_specs=placed, out_specs=P("expert", "section"), check_vma=False
    )
```
